32 devices in a mesh: groups: 2 (over y), tx: 16 (over z, x, core).
Axes of the slice: x: 2, y: 2, z: 4, core: 2. Of those that a mesh axis runs over, the one named last changes fastest.
Arguments:
- mask: bfloat16 [8192, 1024], P(('groups', 'tx')), parts along dimension 0, may hold values from -1 to 1
- kernel_spectra: float32 [2, 96, 12, 128], replicated, may hold values from -3 to 3
- kernel_weights: float32 [12], replicated, may hold values from 0.1 to 1
- threshold: float32 [1], replicated, may hold values from 0.4 to 1.2
- eval_tile: int32 [16384], P(('groups', 'tx')), parts along dimension 0, may hold values from 0 to 15, as said below
- site_coords: float32 [2, 16, 16384], P(None, None, ('groups', 'tx')), parts along dimension 2, may hold values from 0 to 1
- bias_steps: int32 [16384], P(('groups', 'tx')), parts along dimension 0, may hold values from -4 to 4
Outputs:
- resist: float32 [8192, 1024], P(('groups', 'tx')), parts along dimension 0
- new_bias: float32 [16384], P(('groups', 'tx')), parts along dimension 0
The draws below stay inside these ranges and needn't reach their ends.
There are 2 independent parts, one for each index of `groups`. The reference program is written for one: setup_inputs(seed, part) draws one part's arguments, and reference() takes and returns one part's arrays. A program takes and returns all parts, laid end to end along the dimension named above; an argument that names none is the same for every part. Nothing has to cross between parts.
Inputs may be any that keep to these rules, and one draw needn't show every extreme that they name: `eval_tile`: the evaluating tile of a fragment owned by tile t is t - 1, t or t + 1. One owning tile sends at most 256 fragments to each evaluating tile and exactly 256 to at least one of them; in every draw some tile receives exactly 256 fragments from each of the three owners beside it or itself.
All inputs are finite; a program needn't handle non-finite values.
Results may differ from the reference program's by a relative error of at most 0.0019.
Values may be sent and summed in bfloat16 or wider, within the bound.
A program may use at most 64 MiB of HBM per device.

```python
import math
import jax
import jax.numpy as jnp
from jax import lax

ROWS_DEV = 256
COLS = 1024
HALO = 256
BLUR_REACH = 8
KERNELS = 12
SITES = 16
FRAG_DEV = 512
WINDOW = 768
ROW_FREQS = 96
COL_FREQS = 128
REGION_ROWS = 4096
FRAGS = 8192
N_TX = 16


def permuted_order(order_key):
    return jax.random.permutation(order_key, FRAG_DEV)


def draw_eval_tile(key, part):
    tile_total = FRAGS // FRAG_DEV
    capacity = FRAG_DEV // 2
    key_full, key_split, key_dense, key_order = jax.random.split(key, 4)
    owners = jnp.arange(tile_total, dtype=jnp.int32)
    full_side = jax.random.randint(key_full, (tile_total,), 0, 3)
    dense_tile = jax.random.randint(key_dense, (), 1, tile_total - 1)
    full_side = jnp.where(owners == dense_tile - 1, 2, full_side)
    full_side = jnp.where(owners == dense_tile, 1, full_side)
    full_side = jnp.where(owners == dense_tile + 1, 0, full_side)
    split_count = jax.random.randint(key_split, (tile_total,), 0, capacity + 1)
    sides = jnp.arange(3, dtype=jnp.int32)
    is_full = sides[None, :] == full_side[:, None]
    other_rank = jnp.cumsum(1 - is_full.astype(jnp.int32), axis=1) - 1
    counts = jnp.where(is_full, capacity, jnp.where(other_rank == 0, split_count[:, None], capacity - split_count[:, None]))
    first_row = jnp.where(sides == 0, 0, capacity)
    last_row = jnp.where(sides == 2, 0, capacity)
    counts = jnp.where((owners == 0)[:, None], first_row[None, :], counts)
    counts = jnp.where((owners == tile_total - 1)[:, None], last_row[None, :], counts)
    position = jnp.arange(FRAG_DEV, dtype=jnp.int32)
    side_of = (position[None, :] >= counts[:, 0:1]).astype(jnp.int32) + (position[None, :] >= counts[:, 0:1] + counts[:, 1:2]).astype(jnp.int32)
    order_keys = jax.random.split(key_order, tile_total)
    orders = jax.vmap(permuted_order)(order_keys)
    shuffled = jnp.take_along_axis(side_of, orders, axis=1)
    return (owners[:, None] + shuffled - 1).reshape(-1).astype(jnp.int32)


def with_ends(array, stream_key, low, largest):
    index_at = [jax.random.randint(jax.random.fold_in(stream_key, axis), (), 0, length) for axis, length in enumerate(array.shape)]
    widest = array.shape.index(max(array.shape))
    neighbour = index_at[:widest] + [(index_at[widest] + 1) % array.shape[widest]] + index_at[widest + 1:]
    return array.at[tuple(index_at)].set(low).at[tuple(neighbour)].set(largest)


def block_levels(own_key, dims, cuts, smallest, largest):
    def one(dim, parts):
        steps = jax.random.uniform(jax.random.fold_in(jax.random.fold_in(own_key, 6), dim), (parts,), jnp.float32, smallest / len(cuts), largest / len(cuts))
        return jnp.repeat(jnp.exp(steps), dims[dim] // parts).reshape((-1,) + (1,) * (len(dims) - dim - 1))

    factor_of = one(*cuts[0])
    for cut in cuts[1:]:
        factor_of = factor_of * one(*cut)
    return factor_of


def noise(rng, dims, spread, most, held_as=jnp.bfloat16):
    result = jax.random.normal(rng, dims, jnp.float32) * spread
    return jnp.minimum(jnp.maximum(result, -most), most).astype(held_as)


def setup_inputs(seed: int = 0, part: int = 0) -> dict:
    seeds = jax.random.split(jax.random.key(seed), 8)
    own_keys = jax.random.split(jax.random.fold_in(seeds[7], part), 8)
    mask = jnp.clip(jax.random.uniform(own_keys[0], (REGION_ROWS, COLS), jnp.float32, -1.0, 1.0) * block_levels(own_keys[0], (REGION_ROWS, COLS), ((0, 16),), -0.4, 0.0), -1.0, 1.0).astype(jnp.bfloat16)
    kernel_spectra = noise(seeds[1], (2, ROW_FREQS, KERNELS, COL_FREQS), 0.5, 3.0, jnp.float32)
    kernel_weights = jnp.clip(jnp.exp(jax.random.uniform(seeds[2], (KERNELS,), jnp.float32, math.log(0.1), math.log(1.0))), 0.1, 1.0)
    threshold = jnp.clip(jax.random.uniform(seeds[3], (1,), jnp.float32, 0.4, 1.2), 0.4, 1.2)
    eval_tile = draw_eval_tile(jax.random.fold_in(jax.random.fold_in(seeds[7], part), 71), part)
    site_coords = jnp.clip(1.0 * jax.random.uniform(own_keys[5], (2, SITES, FRAGS), jnp.float32) ** block_levels(own_keys[5], (2, SITES, FRAGS), ((2, 16),), -0.2, 0.2), 0.0, 1.0)
    bias_steps = with_ends(jax.random.randint(own_keys[6], (FRAGS,), -4, 5), jax.random.fold_in(own_keys[6], 1), -4, 4).astype(jnp.int32)
    return {"mask": mask, "kernel_spectra": kernel_spectra, "kernel_weights": kernel_weights, "threshold": threshold, "eval_tile": eval_tile, "site_coords": site_coords, "bias_steps": bias_steps}


blur_sigma = 3.0
bias_step = 0.5
bias_gain = 2.0

def twiddle(position, frequency, period, amplitude):
    phase_index = position[:, None] * frequency[None, :] % period
    phase_angle = phase_index.astype(jnp.float32) * (2.0 * math.pi / period)
    return (jnp.cos(phase_angle) * amplitude, jnp.sin(phase_angle) * amplitude)

def centered(count):
    return jnp.arange(count, dtype=jnp.int32) - count // 2

def imaging_tables(tile_rows, tile_cols, window_rows, row_freqs, col_freqs, halo_rows):
    col_cos, col_sin = twiddle(jnp.arange(tile_cols, dtype=jnp.int32), centered(col_freqs), tile_cols, 1.0 / math.sqrt(tile_cols))
    col_forward = jnp.concatenate([col_cos, -col_sin], axis=1).astype(jnp.bfloat16)
    row_cos, row_sin = twiddle(centered(row_freqs), jnp.arange(window_rows, dtype=jnp.int32), window_rows, 1.0 / math.sqrt(window_rows))
    row_forward = jnp.concatenate([row_cos, -row_sin], axis=0).astype(jnp.bfloat16)
    back_cos, back_sin = twiddle(jnp.arange(tile_rows, dtype=jnp.int32) + halo_rows, centered(row_freqs), window_rows, 1.0 / math.sqrt(row_freqs))
    row_inverse = jnp.concatenate([back_cos, back_sin], axis=0).astype(jnp.bfloat16)
    out_cos, out_sin = twiddle(centered(col_freqs), jnp.arange(tile_cols, dtype=jnp.int32), tile_cols, 1.0 / math.sqrt(col_freqs))
    upper_half = jnp.concatenate([out_cos, out_sin], axis=1)
    lower_half = jnp.concatenate([-out_sin, out_cos], axis=1)
    col_inverse = jnp.concatenate([upper_half, lower_half], axis=0).astype(jnp.bfloat16)
    return (col_forward, row_forward, row_inverse, col_inverse)

def tile_intensity(col_spectra, tables, kernel_spectra, kernel_weights):
    row_forward = tables[1]
    row_inverse = tables[2]
    col_inverse = tables[3]
    row_freqs = kernel_spectra.shape[1]
    kernel_count = kernel_spectra.shape[2]
    col_freqs = kernel_spectra.shape[3]
    tile_rows = row_inverse.shape[0] // 2
    tile_cols = col_inverse.shape[1] // 2
    row_product = jnp.dot(row_forward, col_spectra, preferred_element_type=jnp.float32)
    spec_real = row_product[:row_freqs, :col_freqs] - row_product[row_freqs:, col_freqs:]
    spec_imag = row_product[:row_freqs, col_freqs:] + row_product[row_freqs:, :col_freqs]
    kern_real = kernel_spectra[0]
    kern_imag = kernel_spectra[1]
    prod_real = (kern_real * spec_real[:, None, :] - kern_imag * spec_imag[:, None, :]).astype(jnp.bfloat16)
    prod_imag = (kern_real * spec_imag[:, None, :] + kern_imag * spec_real[:, None, :]).astype(jnp.bfloat16)
    flat_width = kernel_count * col_freqs
    joined = jnp.concatenate([prod_real.reshape(row_freqs, flat_width), prod_imag.reshape(row_freqs, flat_width)], axis=1)
    back_product = jnp.dot(row_inverse, joined, preferred_element_type=jnp.float32)
    half_real = (back_product[:tile_rows, :flat_width] - back_product[tile_rows:, flat_width:]).astype(jnp.bfloat16)
    half_imag = (back_product[:tile_rows, flat_width:] + back_product[tile_rows:, :flat_width]).astype(jnp.bfloat16)
    stacked = jnp.concatenate([half_real.reshape(tile_rows, kernel_count, col_freqs), half_imag.reshape(tile_rows, kernel_count, col_freqs)], axis=2)
    stacked = jnp.transpose(stacked, (1, 0, 2))

    def add_kernel(intensity_sum, inputs):
        kernel_block, kernel_weight = inputs
        field_pair = jnp.dot(kernel_block, col_inverse, preferred_element_type=jnp.float32)
        field_real = field_pair[:, :tile_cols]
        field_imag = field_pair[:, tile_cols:]
        return (intensity_sum + kernel_weight * (field_real * field_real + field_imag * field_imag), None)
    start_sum = jnp.zeros((tile_rows, tile_cols), jnp.float32)
    intensity_sum, unused_out = lax.scan(add_kernel, start_sum, (stacked, kernel_weights))
    return intensity_sum.astype(jnp.bfloat16)

def blur_weight(offset, reach):
    offset_value = offset.astype(jnp.float32)
    all_offsets = jnp.arange(-reach, reach + 1, dtype=jnp.int32).astype(jnp.float32)
    norm_sum = jnp.sum(jnp.exp(-all_offsets * all_offsets / (2.0 * blur_sigma * blur_sigma)))
    inside = jnp.abs(offset) <= reach
    return jnp.where(inside, jnp.exp(-offset_value * offset_value / (2.0 * blur_sigma * blur_sigma)) / norm_sum, jnp.float32(0.0))

def blur_tables(tile_rows, tile_cols, reach):
    col_diff = jnp.arange(tile_cols, dtype=jnp.int32)[None, :] - jnp.arange(tile_cols, dtype=jnp.int32)[:, None]
    col_blur = blur_weight(col_diff, reach).astype(jnp.bfloat16)
    row_diff = jnp.arange(tile_rows + 2 * reach, dtype=jnp.int32)[None, :] - reach - jnp.arange(tile_rows, dtype=jnp.int32)[:, None]
    row_blur = blur_weight(row_diff, reach).astype(jnp.bfloat16)
    return (col_blur, row_blur)

def sample_resist(resist, row_frac, col_frac, row_base, tile_rows):
    tile_cols = resist.shape[1]
    row_pos = row_frac * (tile_rows - 1)
    col_pos = col_frac * (tile_cols - 1)
    row_low = jnp.minimum(jnp.floor(row_pos), tile_rows - 2)
    col_low = jnp.minimum(jnp.floor(col_pos), tile_cols - 2)
    row_part = row_pos - row_low
    col_part = col_pos - col_low
    first_index = (row_low.astype(jnp.int32) + row_base) * tile_cols + col_low.astype(jnp.int32)
    flat_resist = resist.reshape(-1)
    upper_left = flat_resist[first_index]
    upper_right = flat_resist[first_index + 1]
    lower_left = flat_resist[first_index + tile_cols]
    lower_right = flat_resist[first_index + tile_cols + 1]
    top_line = (1.0 - col_part) * upper_left + col_part * upper_right
    bottom_line = (1.0 - col_part) * lower_left + col_part * lower_right
    return (1.0 - row_part) * top_line + row_part * bottom_line

def reference(mask, kernel_spectra, kernel_weights, threshold, eval_tile, site_coords, bias_steps):
    tables = imaging_tables(ROWS_DEV, COLS, WINDOW, ROW_FREQS, COL_FREQS, HALO)
    padded_mask = jnp.pad(mask, ((HALO, HALO), (0, 0)))

    def one_tile(tile_index):
        window = lax.dynamic_slice_in_dim(padded_mask, (tile_index * ROWS_DEV).astype(jnp.int32), WINDOW, 0)
        col_spectra = jnp.dot(window, tables[0], preferred_element_type=jnp.float32).astype(jnp.bfloat16)
        return tile_intensity(col_spectra, tables, kernel_spectra, kernel_weights)
    tile_numbers = jnp.arange(N_TX, dtype=jnp.int32)
    intensity = lax.map(one_tile, tile_numbers).reshape(REGION_ROWS, COLS)
    col_blur, row_blur = blur_tables(ROWS_DEV, COLS, BLUR_REACH)
    padded_intensity = jnp.pad(intensity, ((BLUR_REACH, BLUR_REACH), (0, 0)))
    col_blurred = jnp.dot(padded_intensity, col_blur, preferred_element_type=jnp.float32).astype(jnp.bfloat16)

    def blur_tile(tile_index):
        row_block = lax.dynamic_slice_in_dim(col_blurred, (tile_index * ROWS_DEV).astype(jnp.int32), ROWS_DEV + 2 * BLUR_REACH, 0)
        return jnp.dot(row_blur, row_block, preferred_element_type=jnp.float32)
    resist = lax.map(blur_tile, tile_numbers).reshape(REGION_ROWS, COLS)
    site_values = sample_resist(resist, site_coords[0], site_coords[1], eval_tile[None, :] * ROWS_DEV, ROWS_DEV)
    site_mean = lax.optimization_barrier(jnp.mean(site_values, axis=0))
    new_bias = bias_step * bias_steps.astype(jnp.float32) - bias_gain * (site_mean - threshold[0])
    return (resist, new_bias)
```

```python
import math

import jax
import jax.numpy as jnp
import ml_dtypes
import numpy as np
from jax import lax
from jax.experimental import pallas as pl
from jax.experimental.pallas import tpu as pltpu
from jax.sharding import PartitionSpec as P

HALO = 256
REACH = 8
SITES = 16
GRID_STEP = 4
BLOCK = 64
SIGMA = 3.0
BF = jnp.bfloat16
F32 = jnp.float32
MESH = pl.DeviceIdType.MESH


def host_bf16(x):
    return np.asarray(x, np.float32).astype(ml_dtypes.bfloat16)


def twiddle(position, frequency, period, amplitude):
    index = (position[:, None] * frequency[None, :]) % period
    angle = index.astype(np.float64) * (2.0 * math.pi / period)
    return np.cos(angle) * amplitude, np.sin(angle) * amplitude


def gauss(offset):
    every = np.arange(-REACH, REACH + 1)
    norm = np.sum(np.exp(-every * every / (2.0 * SIGMA * SIGMA)))
    value = np.exp(-offset * offset / (2.0 * SIGMA * SIGMA)) / norm
    return np.where(np.abs(offset) <= REACH, value, 0.0)


def split2(x):
    high = host_bf16(x)
    low = host_bf16(x - high.astype(np.float64))
    return high, low


def tables(rows, cols, row_freqs, col_freqs):
    window = rows + 2 * HALO
    f = np.arange(col_freqs) - col_freqs // 2
    g = np.arange(row_freqs) - row_freqs // 2
    c, s = twiddle(np.arange(cols), f, cols, 1.0 / math.sqrt(cols))
    col_forward = host_bf16(np.concatenate([c, -s], 1))
    c, s = twiddle(g, np.arange(window), window, 1.0 / math.sqrt(window))
    row_forward = host_bf16(np.concatenate([c, -s], 0))
    c, s = twiddle(np.arange(rows) + HALO, g, window, 1.0 / math.sqrt(row_freqs))
    row_inverse = host_bf16(np.block([[c, -s], [s, c]]))
    picked = np.arange(0, cols, GRID_STEP)
    c, s = twiddle(f, picked, cols, 1.0 / math.sqrt(col_freqs))
    col_inverse = host_bf16(np.block([[c, s], [-s, c]]))
    diff = np.arange(cols)[None, :] - picked[:, None]
    order = np.arange(1, col_freqs)
    base = np.arange(cols)
    kernel = 1.0 + 2.0 * np.cos(2 * math.pi * ((base[:, None] * order[None, :]) % cols) / cols).sum(1)
    kernel = (kernel + np.cos(2 * math.pi * ((base * col_freqs) % cols) / cols)) / picked.size
    interp = kernel[diff % cols]
    lines = np.arange(cols)
    col_blur = host_bf16(gauss((lines[None, :] - lines[:, None]).astype(np.float64)))
    spread = interp @ col_blur.astype(np.float64)
    high, low = split2(spread)
    wide = np.concatenate([high, low], 0)
    row_diff = np.arange(rows + 2 * REACH)[None, :] - REACH - np.arange(rows)[:, None]
    row_blur = host_bf16(gauss(row_diff.astype(np.float64)))
    row_mid = np.ascontiguousarray(row_blur[:, REACH:REACH + rows])
    row_edge = np.concatenate([row_blur[:, :REACH], row_blur[:, REACH + rows:]], 1)
    return (col_forward, row_forward, row_inverse, col_inverse, row_mid, row_edge, wide,
            np.ascontiguousarray(high.T))


def dot(a, b):
    return jnp.dot(a, b, preferred_element_type=F32)


def dot_nt(a, b):
    return lax.dot_general(a, b, (((1,), (1,)), ((), ())), preferred_element_type=F32)


def split3(x):
    high = x.astype(BF)
    rest = x - high.astype(F32)
    mid = rest.astype(BF)
    low = (rest - mid.astype(F32)).astype(BF)
    return jnp.concatenate([high, mid, low], axis=0)


def hat(distance):
    return jnp.maximum(1.0 - jnp.abs(distance), 0.0)


def kernel(mask, spectra, weights, thresh, ev, sc, bias, colf, rowf, rinv, cinv, rmid, redge,
           wide_h, wide_t_h, resist_h, nb,
           win, snd, recs, inten, hsnd, halo, rsnd, ret, sel, ksv, wide, wide_t, resist, rt,
           local_sem, send_sem, recv_sem):
    t = lax.axis_index("tx")
    count = lax.axis_size("tx")
    has_left = t > 0
    has_right = t < count - 1
    rows, cols = mask.shape
    row_freqs, kernels, col_freqs = ksv.shape[1:]
    frags = ev.shape[1]
    cap = frags // 2

    barrier = pltpu.get_barrier_semaphore()

    @pl.when(has_left)
    def _():
        pl.semaphore_signal(barrier, inc=1, device_id={"tx": t - 1}, device_id_type=MESH)

    @pl.when(has_right)
    def _():
        pl.semaphore_signal(barrier, inc=1, device_id={"tx": t + 1}, device_id_type=MESH)

    load_ks = pltpu.make_async_copy(spectra, ksv, local_sem.at[0])
    load_wide = pltpu.make_async_copy(wide_h, wide, local_sem.at[1])
    load_wide_t = pltpu.make_async_copy(wide_t_h, wide_t, local_sem.at[2])
    load_ks.start()
    load_wide.start()
    load_wide_t.start()

    def to_left(kind, src, dst):
        return pltpu.make_async_remote_copy(
            src_ref=src, dst_ref=dst, send_sem=send_sem.at[kind, 0], recv_sem=recv_sem.at[kind, 0],
            device_id={"tx": t - 1}, device_id_type=MESH)

    def to_right(kind, src, dst):
        return pltpu.make_async_remote_copy(
            src_ref=src, dst_ref=dst, send_sem=send_sem.at[kind, 1], recv_sem=recv_sem.at[kind, 1],
            device_id={"tx": t + 1}, device_id_type=MESH)

    own = win.at[pl.ds(HALO, rows)]
    pairs = (
        (to_left(0, own, win.at[pl.ds(HALO + rows, HALO)]), to_right(0, own, win.at[pl.ds(0, HALO)])),
        (to_left(1, snd.at[0], recs.at[2]), to_right(1, snd.at[2], recs.at[0])),
        (to_left(2, hsnd.at[0], halo.at[1]), to_right(2, hsnd.at[1], halo.at[0])),
        (to_left(3, rsnd.at[0], ret.at[2]), to_right(3, rsnd.at[2], ret.at[0])),
    )

    def start(kind):
        @pl.when(has_left)
        def _():
            pairs[kind][0].start()

        @pl.when(has_right)
        def _():
            pairs[kind][1].start()

    def arrive(kind):
        @pl.when(has_right)
        def _():
            pairs[kind][0].wait_recv()

        @pl.when(has_left)
        def _():
            pairs[kind][1].wait_recv()

    @pl.when(jnp.logical_not(has_left))
    def _():
        win[0:HALO] = jnp.zeros((HALO, win.shape[1]), BF)
        recs[0] = jnp.zeros(recs.shape[1:], F32)
        halo[0] = jnp.zeros(halo.shape[1:], F32)
        ret[0] = jnp.zeros(ret.shape[1:], F32)

    @pl.when(jnp.logical_not(has_right))
    def _():
        win[HALO + rows:] = jnp.zeros((HALO, win.shape[1]), BF)
        recs[2] = jnp.zeros(recs.shape[1:], F32)
        halo[1] = jnp.zeros(halo.shape[1:], F32)
        ret[2] = jnp.zeros(ret.shape[1:], F32)

    win[HALO:HALO + rows] = dot(mask[...], colf[...]).astype(BF)

    between = jnp.logical_and(has_left, has_right)

    @pl.when(between)
    def _():
        pl.semaphore_wait(barrier, 2)

    @pl.when(jnp.logical_not(between))
    def _():
        pl.semaphore_wait(barrier, 1)

    start(0)

    offset = ev[...] - t + 1
    member = jnp.where(lax.broadcasted_iota(jnp.int32, (8, frags), 0) == offset, 1.0, 0.0)
    upper = jnp.where(
        lax.broadcasted_iota(jnp.int32, (frags, frags), 0)
        <= lax.broadcasted_iota(jnp.int32, (frags, frags), 1), 1.0, 0.0).astype(BF)
    inclusive = dot(member.astype(BF), upper)
    rank = jnp.sum(member * (inclusive - 1.0), axis=0, keepdims=True)
    slot = offset.astype(F32) * float(cap) + rank
    slot_line = lax.broadcasted_iota(jnp.int32, (3 * cap, frags), 0).astype(F32)
    sel[...] = jnp.where(slot_line == slot, 1.0, 0.0).astype(BF)
    records = jnp.concatenate([sc[0], sc[1]], axis=0)
    packed = dot_nt(split3(records), sel[...])
    n_rec = 2 * SITES
    packed = packed[:n_rec] + packed[n_rec:2 * n_rec] + packed[2 * n_rec:]
    snd[0] = packed[:, :cap]
    recs[1] = packed[:, cap:2 * cap]
    snd[2] = packed[:, 2 * cap:]
    start(1)

    product = dot(rowf[:, HALO:HALO + rows], win[HALO:HALO + rows])
    load_ks.wait()
    arrive(0)
    product = product + dot(rowf[:, :HALO], win[:HALO]) + dot(rowf[:, HALO + rows:], win[HALO + rows:])
    real = product[:row_freqs, :col_freqs] - product[row_freqs:, col_freqs:]
    imag = product[:row_freqs, col_freqs:] + product[row_freqs:, :col_freqs]

    total = jnp.zeros((rows, cinv.shape[1] // 2), F32)
    half = cinv.shape[1] // 2
    for pair in range(kernels // 2):
        blocks = []
        for k in (2 * pair, 2 * pair + 1):
            kr = ksv[0, :, k, :]
            ki = ksv[1, :, k, :]
            blocks.append(jnp.concatenate(
                [(kr * real - ki * imag).astype(BF), (kr * imag + ki * real).astype(BF)], axis=0))
        field = dot(rinv[...], jnp.concatenate(blocks, axis=1)).astype(BF)
        for i in range(2):
            part = field[:, i * col_freqs:(i + 1) * col_freqs]
            e = dot(jnp.concatenate([part[:rows], part[rows:]], axis=1), cinv[...])
            er = e[:, :half]
            ei = e[:, half:]
            total = total + weights[2 * pair + i] * (er * er + ei * ei)

    rounded = total.astype(BF)
    inten[...] = rounded
    hsnd[0] = rounded[:REACH].astype(F32)
    hsnd[1] = rounded[rows - REACH:].astype(F32)
    start(2)
    blurred = dot(rmid[...], inten[...])
    arrive(2)
    edge = jnp.concatenate([halo[0], halo[1]], axis=0).astype(BF)
    blurred = blurred + dot(redge[...], edge)
    center = jnp.sum(blurred) * (1.0 / (blurred.shape[0] * blurred.shape[1]))
    high = blurred.astype(BF)
    low = (blurred - high.astype(F32)).astype(BF)
    load_wide_t.wait()
    rt[...] = (dot_nt(wide_t[...], high) + dot_nt(wide_t[...], low) - center).astype(BF)
    load_wide.wait()
    coarse = high.shape[1]
    resist[...] = (dot(high, wide[:coarse]) + dot(low, wide[:coarse])) + dot(high, wide[coarse:])
    store = pltpu.make_async_copy(resist, resist_h, local_sem.at[3])
    store.start()
    arrive(1)

    blocks_n = cols // BLOCK
    row_line = lax.broadcasted_iota(jnp.int32, (rows, cap), 0).astype(F32)
    col_line = lax.broadcasted_iota(jnp.int32, (BLOCK, cap), 0).astype(F32)
    end_line = lax.broadcasted_iota(jnp.int32, (8, cap), 0).astype(F32) + float(BLOCK)

    def evaluate(block):
        def one(s, acc):
            p = recs[block, pl.ds(s, 1), :] * float(rows - 1)
            q = recs[block, pl.ds(SITES + s, 1), :] * float(cols - 1)
            wr = hat(row_line - p).astype(BF)
            lines = dot(rt[...], wr)
            h = jnp.floor(q * (1.0 / BLOCK))
            local = q - h * float(BLOCK)
            chosen = lines[:BLOCK]
            after = jnp.zeros((8, cap), F32)
            for k in range(1, blocks_n):
                here = lines[k * BLOCK:(k + 1) * BLOCK]
                chosen = jnp.where(h == float(k), here, chosen)
                after = jnp.where(h == float(k - 1), here[:8], after)
            weighted = chosen * hat(col_line - local)
            for g in range(BLOCK // 8):
                acc = acc + weighted[g * 8:(g + 1) * 8]
            return acc + after * hat(end_line - local)

        def step(i, acc):
            return one(2 * i + 1, one(2 * i, acc))

        acc = lax.fori_loop(0, SITES // 2, step, jnp.zeros((8, cap), F32))
        mean = jnp.sum(acc, axis=0, keepdims=True) * (1.0 / SITES) + center
        return jnp.broadcast_to(mean, (8, cap))

    rsnd[0] = evaluate(0)
    rsnd[2] = evaluate(2)
    start(3)
    ret[1] = evaluate(1)
    arrive(3)
    back = jnp.concatenate([ret[0], ret[1], ret[2]], axis=1)
    found = dot(split3(back), sel[...])
    mean = found[0:1] + found[8:9] + found[16:17]
    nb[...] = 0.5 * bias[...].astype(F32) - 2.0 * (mean - thresh[0])

    for kind in range(4):
        @pl.when(has_left)
        def _():
            pairs[kind][0].wait_send()

        @pl.when(has_right)
        def _():
            pairs[kind][1].wait_send()
    store.wait()


def shards(mask, kernel_spectra, kernel_weights, threshold, eval_tile, site_coords, bias_steps):
    rows, cols = mask.shape
    row_freqs, kernels, col_freqs = kernel_spectra.shape[1:]
    frags = eval_tile.shape[0]
    cap = frags // 2
    made = [jnp.asarray(x) for x in tables(rows, cols, row_freqs, col_freqs)]
    vmem = pl.BlockSpec(memory_space=pltpu.VMEM)
    smem = pl.BlockSpec(memory_space=pltpu.SMEM)
    anywhere = pl.BlockSpec(memory_space=pl.ANY)
    coarse = cols // GRID_STEP
    resist, new_bias = pl.pallas_call(
        kernel,
        out_shape=(jax.ShapeDtypeStruct((rows, cols), F32), jax.ShapeDtypeStruct((1, frags), F32)),
        in_specs=[vmem, anywhere, smem, smem, vmem, vmem, vmem] + [vmem] * 6 + [anywhere] * 2,
        out_specs=(anywhere, vmem),
        scratch_shapes=[
            pltpu.VMEM((rows + 2 * HALO, 2 * col_freqs), BF),
            pltpu.VMEM((3, 2 * SITES, cap), F32),
            pltpu.VMEM((3, 2 * SITES, cap), F32),
            pltpu.VMEM((rows, coarse), BF),
            pltpu.VMEM((2, REACH, coarse), F32),
            pltpu.VMEM((2, REACH, coarse), F32),
            pltpu.VMEM((3, 8, cap), F32),
            pltpu.VMEM((3, 8, cap), F32),
            pltpu.VMEM((3 * cap, frags), BF),
            pltpu.VMEM(kernel_spectra.shape, F32),
            pltpu.VMEM((2 * coarse, cols), BF),
            pltpu.VMEM((cols, coarse), BF),
            pltpu.VMEM((rows, cols), F32),
            pltpu.VMEM((cols, rows), BF),
            pltpu.SemaphoreType.DMA((4,)),
            pltpu.SemaphoreType.DMA((4, 2)),
            pltpu.SemaphoreType.DMA((4, 2)),
        ],
        compiler_params=pltpu.CompilerParams(
            collective_id=0, has_side_effects=True, vmem_limit_bytes=48 << 20),
    )(mask, kernel_spectra, kernel_weights, threshold, eval_tile.reshape(1, frags), site_coords,
      bias_steps.reshape(1, frags), *made)
    return resist, new_bias.reshape(frags)


def solution(mesh):
    placed = (
        P(("groups", "tx"), None),
        P(),
        P(),
        P(),
        P(("groups", "tx")),
        P(None, None, ("groups", "tx")),
        P(("groups", "tx")),
    )
    return jax.shard_map(
        shards,
        mesh=mesh,
        in_specs=placed,
        out_specs=(P(("groups", "tx"), None), P(("groups", "tx"))),
        check_vma=False,
    )
```

```python
import math

import jax
import jax.numpy as jnp
import ml_dtypes
import numpy as np
from jax import lax
from jax.experimental import pallas as pl
from jax.experimental.pallas import tpu as pltpu
from jax.sharding import PartitionSpec as P

HALO = 256
REACH = 8
SITES = 16
GRID_STEP = 4
BLOCK = 64
SIGMA = 3.0
BF = jnp.bfloat16
F32 = jnp.float32
MESH = pl.DeviceIdType.MESH
LOADED = ("mask", "colf", "ev", "sc", "rowf", "ks", "rinv", "cinv", "rmid", "redge", "wide_t", "wide")


def host_bf16(x):
    return np.asarray(x, np.float32).astype(ml_dtypes.bfloat16)


def twiddle(position, frequency, period, amplitude):
    index = (position[:, None] * frequency[None, :]) % period
    angle = index.astype(np.float64) * (2.0 * math.pi / period)
    return np.cos(angle) * amplitude, np.sin(angle) * amplitude


def gauss(offset):
    every = np.arange(-REACH, REACH + 1)
    norm = np.sum(np.exp(-every * every / (2.0 * SIGMA * SIGMA)))
    value = np.exp(-offset * offset / (2.0 * SIGMA * SIGMA)) / norm
    return np.where(np.abs(offset) <= REACH, value, 0.0)


def split2(x):
    high = host_bf16(x)
    low = host_bf16(x - high.astype(np.float64))
    return high, low


def tables(rows, cols, row_freqs, col_freqs):
    window = rows + 2 * HALO
    f = np.arange(col_freqs) - col_freqs // 2
    g = np.arange(row_freqs) - row_freqs // 2
    c, s = twiddle(np.arange(cols), f, cols, 1.0 / math.sqrt(cols))
    col_forward = host_bf16(np.concatenate([c, -s], 1))
    c, s = twiddle(g, np.arange(window), window, 1.0 / math.sqrt(window))
    row_forward = host_bf16(np.concatenate([c, -s], 0))
    c, s = twiddle(np.arange(rows) + HALO, g, window, 1.0 / math.sqrt(row_freqs))
    row_inverse = host_bf16(np.block([[c, -s], [s, c]]))
    picked = np.arange(0, cols, GRID_STEP)
    c, s = twiddle(f, picked, cols, 1.0 / math.sqrt(col_freqs))
    col_inverse = host_bf16(np.block([[c, s], [-s, c]]))
    diff = np.arange(cols)[None, :] - picked[:, None]
    order = np.arange(1, col_freqs)
    base = np.arange(cols)
    kernel = 1.0 + 2.0 * np.cos(2 * math.pi * ((base[:, None] * order[None, :]) % cols) / cols).sum(1)
    kernel = (kernel + np.cos(2 * math.pi * ((base * col_freqs) % cols) / cols)) / picked.size
    interp = kernel[diff % cols]
    lines = np.arange(cols)
    col_blur = host_bf16(gauss((lines[None, :] - lines[:, None]).astype(np.float64)))
    spread = interp @ col_blur.astype(np.float64)
    high, low = split2(spread)
    wide = np.concatenate([high, low], 0)
    row_diff = np.arange(rows + 2 * REACH)[None, :] - REACH - np.arange(rows)[:, None]
    row_blur = host_bf16(gauss(row_diff.astype(np.float64)))
    row_mid = np.ascontiguousarray(row_blur[:, REACH:REACH + rows])
    row_edge = np.concatenate([row_blur[:, :REACH], row_blur[:, REACH + rows:]], 1)
    return (col_forward, row_forward, row_inverse, col_inverse, row_mid, row_edge, wide,
            np.ascontiguousarray(high.T))


def dot(a, b):
    return jnp.dot(a, b, preferred_element_type=F32)


def dot_nt(a, b):
    return lax.dot_general(a, b, (((1,), (1,)), ((), ())), preferred_element_type=F32)


def split3(x):
    high = x.astype(BF)
    rest = x - high.astype(F32)
    mid = rest.astype(BF)
    low = (rest - mid.astype(F32)).astype(BF)
    return jnp.concatenate([high, mid, low], axis=0)


def hat(distance):
    return jnp.maximum(1.0 - jnp.abs(distance), 0.0)


def kernel(weights_h, *refs):
    n = len(LOADED)
    sources = dict(zip(LOADED, refs[:n]))
    resist_h, mean_out = refs[n:n + 2]
    held = dict(zip(LOADED, refs[n + 2:2 * n + 2]))
    (weights, win, snd, recs, inten, hsnd, halo, rsnd, ret, sel, resist, rt,
     local_sem, send_sem, recv_sem) = refs[2 * n + 2:]
    mask, colf, ev, sc, rowf, ksv, rinv, cinv, rmid, redge, wide_t, wide = (held[k] for k in LOADED)
    t = lax.axis_index("tx")
    count = lax.axis_size("tx")
    has_left = t > 0
    has_right = t < count - 1
    rows, cols = mask.shape
    kernels, row_freqs, col_freqs = ksv.shape[1:]
    frags = ev.shape[1]
    cap = frags // 2

    barrier = pltpu.get_barrier_semaphore()

    @pl.when(has_left)
    def _():
        pl.semaphore_signal(barrier, inc=1, device_id={"tx": t - 1}, device_id_type=MESH)

    @pl.when(has_right)
    def _():
        pl.semaphore_signal(barrier, inc=1, device_id={"tx": t + 1}, device_id_type=MESH)

    loads = {k: pltpu.make_async_copy(sources[k], held[k], local_sem.at[i])
             for i, k in enumerate(LOADED)}
    for k in LOADED:
        loads[k].start()
    load_weights = pltpu.make_async_copy(weights_h, weights, local_sem.at[n])
    load_weights.start()

    def to_left(kind, src, dst):
        return pltpu.make_async_remote_copy(
            src_ref=src, dst_ref=dst, send_sem=send_sem.at[kind, 0], recv_sem=recv_sem.at[kind, 0],
            device_id={"tx": t - 1}, device_id_type=MESH)

    def to_right(kind, src, dst):
        return pltpu.make_async_remote_copy(
            src_ref=src, dst_ref=dst, send_sem=send_sem.at[kind, 1], recv_sem=recv_sem.at[kind, 1],
            device_id={"tx": t + 1}, device_id_type=MESH)

    own = win.at[pl.ds(HALO, rows)]
    pairs = (
        (to_left(0, own, win.at[pl.ds(HALO + rows, HALO)]), to_right(0, own, win.at[pl.ds(0, HALO)])),
        (to_left(1, snd.at[0], recs.at[2]), to_right(1, snd.at[2], recs.at[0])),
        (to_left(2, hsnd.at[0], halo.at[1]), to_right(2, hsnd.at[1], halo.at[0])),
        (to_left(3, rsnd.at[0], ret.at[2]), to_right(3, rsnd.at[2], ret.at[0])),
    )

    def start(kind):
        @pl.when(has_left)
        def _():
            pairs[kind][0].start()

        @pl.when(has_right)
        def _():
            pairs[kind][1].start()

    def arrive(kind):
        @pl.when(has_right)
        def _():
            pairs[kind][0].wait_recv()

        @pl.when(has_left)
        def _():
            pairs[kind][1].wait_recv()

    @pl.when(jnp.logical_not(has_left))
    def _():
        win[0:HALO] = jnp.zeros((HALO, win.shape[1]), BF)
        recs[0] = jnp.zeros(recs.shape[1:], F32)
        halo[0] = jnp.zeros(halo.shape[1:], F32)
        ret[0] = jnp.zeros(ret.shape[1:], F32)

    @pl.when(jnp.logical_not(has_right))
    def _():
        win[HALO + rows:] = jnp.zeros((HALO, win.shape[1]), BF)
        recs[2] = jnp.zeros(recs.shape[1:], F32)
        halo[1] = jnp.zeros(halo.shape[1:], F32)
        ret[2] = jnp.zeros(ret.shape[1:], F32)

    loads["mask"].wait()
    loads["colf"].wait()
    win[HALO:HALO + rows] = dot(mask[...], colf[...]).astype(BF)

    between = jnp.logical_and(has_left, has_right)

    @pl.when(between)
    def _():
        pl.semaphore_wait(barrier, 2)

    @pl.when(jnp.logical_not(between))
    def _():
        pl.semaphore_wait(barrier, 1)

    start(0)

    loads["ev"].wait()
    loads["sc"].wait()
    offset = ev[...] - t + 1
    member = jnp.where(lax.broadcasted_iota(jnp.int32, (8, frags), 0) == offset, 1.0, 0.0)
    upper = jnp.where(
        lax.broadcasted_iota(jnp.int32, (frags, frags), 0)
        <= lax.broadcasted_iota(jnp.int32, (frags, frags), 1), 1.0, 0.0).astype(BF)
    inclusive = dot(member.astype(BF), upper)
    rank = jnp.sum(member * (inclusive - 1.0), axis=0, keepdims=True)
    slot = offset.astype(F32) * float(cap) + rank
    slot_line = lax.broadcasted_iota(jnp.int32, (3 * cap, frags), 0).astype(F32)
    sel[...] = jnp.where(slot_line == slot, 1.0, 0.0).astype(BF)
    records = jnp.concatenate([sc[0], sc[1]], axis=0)
    packed = dot_nt(split3(records), sel[...])
    n_rec = 2 * SITES
    packed = packed[:n_rec] + packed[n_rec:2 * n_rec] + packed[2 * n_rec:]
    snd[0] = packed[:, :cap]
    recs[1] = packed[:, cap:2 * cap]
    snd[2] = packed[:, 2 * cap:]
    start(1)

    loads["rowf"].wait()
    product = dot(rowf[:, HALO:HALO + rows], win[HALO:HALO + rows])
    for k in ("ks", "rinv", "cinv", "rmid", "redge"):
        loads[k].wait()
    load_weights.wait()
    arrive(0)
    product = product + dot(rowf[:, :HALO], win[:HALO]) + dot(rowf[:, HALO + rows:], win[HALO + rows:])
    real = product[:row_freqs, :col_freqs] - product[row_freqs:, col_freqs:]
    imag = product[:row_freqs, col_freqs:] + product[row_freqs:, :col_freqs]

    total = jnp.zeros((rows, cinv.shape[1] // 2), F32)
    half = cinv.shape[1] // 2
    for pair in range(kernels // 2):
        blocks = []
        for k in (2 * pair, 2 * pair + 1):
            kr = ksv[0, k]
            ki = ksv[1, k]
            blocks.append(jnp.concatenate(
                [(kr * real - ki * imag).astype(BF), (kr * imag + ki * real).astype(BF)], axis=0))
        field = dot(rinv[...], jnp.concatenate(blocks, axis=1)).astype(BF)
        for i in range(2):
            part = field[:, i * col_freqs:(i + 1) * col_freqs]
            e = dot(jnp.concatenate([part[:rows], part[rows:]], axis=1), cinv[...])
            er = e[:, :half]
            ei = e[:, half:]
            total = total + weights[2 * pair + i] * (er * er + ei * ei)

    rounded = total.astype(BF)
    inten[...] = rounded
    hsnd[0] = rounded[:REACH].astype(F32)
    hsnd[1] = rounded[rows - REACH:].astype(F32)
    start(2)
    blurred = dot(rmid[...], inten[...])
    arrive(2)
    edge = jnp.concatenate([halo[0], halo[1]], axis=0).astype(BF)
    blurred = blurred + dot(redge[...], edge)
    center = jnp.sum(blurred) * (1.0 / (blurred.shape[0] * blurred.shape[1]))
    high = blurred.astype(BF)
    low = (blurred - high.astype(F32)).astype(BF)
    loads["wide_t"].wait()
    rt[...] = (dot_nt(wide_t[...], high) + dot_nt(wide_t[...], low) - center).astype(BF)
    loads["wide"].wait()
    coarse = high.shape[1]
    resist[...] = (dot(high, wide[:coarse]) + dot(low, wide[:coarse])) + dot(high, wide[coarse:])
    store = pltpu.make_async_copy(resist, resist_h, local_sem.at[n + 1])
    store.start()
    arrive(1)

    blocks_n = cols // BLOCK
    row_line = lax.broadcasted_iota(jnp.int32, (rows, cap), 0).astype(F32)
    col_line = lax.broadcasted_iota(jnp.int32, (BLOCK, cap), 0).astype(F32)
    end_line = lax.broadcasted_iota(jnp.int32, (8, cap), 0).astype(F32) + float(BLOCK)

    def evaluate(block):
        def one(s, acc):
            p = recs[block, pl.ds(s, 1), :] * float(rows - 1)
            q = recs[block, pl.ds(SITES + s, 1), :] * float(cols - 1)
            wr = hat(row_line - p).astype(BF)
            lines = dot(rt[...], wr)
            h = jnp.floor(q * (1.0 / BLOCK))
            local = q - h * float(BLOCK)
            chosen = lines[:BLOCK]
            after = jnp.zeros((8, cap), F32)
            for k in range(1, blocks_n):
                here = lines[k * BLOCK:(k + 1) * BLOCK]
                chosen = jnp.where(h == float(k), here, chosen)
                after = jnp.where(h == float(k - 1), here[:8], after)
            weighted = chosen * hat(col_line - local)
            for g in range(BLOCK // 8):
                acc = acc + weighted[g * 8:(g + 1) * 8]
            return acc + after * hat(end_line - local)

        def step(i, acc):
            return one(2 * i + 1, one(2 * i, acc))

        acc = lax.fori_loop(0, SITES // 2, step, jnp.zeros((8, cap), F32))
        mean = jnp.sum(acc, axis=0, keepdims=True) * (1.0 / SITES) + center
        return jnp.broadcast_to(mean, (8, cap))

    rsnd[0] = evaluate(0)
    rsnd[2] = evaluate(2)
    start(3)
    ret[1] = evaluate(1)
    arrive(3)
    back = jnp.concatenate([ret[0], ret[1], ret[2]], axis=1)
    found = dot(split3(back), sel[...])
    mean_out[...] = (found[0:1] + found[8:9] + found[16:17]).reshape(frags)

    for kind in range(4):
        @pl.when(has_left)
        def _():
            pairs[kind][0].wait_send()

        @pl.when(has_right)
        def _():
            pairs[kind][1].wait_send()
    store.wait()


def shards(mask, kernel_spectra, kernel_weights, threshold, eval_tile, site_coords, bias_steps):
    rows, cols = mask.shape
    row_freqs, kernels, col_freqs = kernel_spectra.shape[1:]
    frags = eval_tile.shape[0]
    cap = frags // 2
    names = ("colf", "rowf", "rinv", "cinv", "rmid", "redge", "wide", "wide_t")
    values = dict(zip(names, (jnp.asarray(x) for x in tables(rows, cols, row_freqs, col_freqs))))
    values["mask"] = mask
    values["ks"] = jnp.transpose(kernel_spectra, (0, 2, 1, 3))
    values["ev"] = eval_tile.reshape(1, frags)
    values["sc"] = site_coords
    ordered = [values[k] for k in LOADED]
    vmem = pl.BlockSpec(memory_space=pltpu.VMEM)
    hbm = pl.BlockSpec(memory_space=pltpu.HBM)
    coarse = cols // GRID_STEP
    resist, mean = pl.pallas_call(
        kernel,
        out_shape=(jax.ShapeDtypeStruct((rows, cols), F32), jax.ShapeDtypeStruct((frags,), F32)),
        in_specs=[hbm] * (1 + len(ordered)),
        out_specs=(pl.BlockSpec(memory_space=pl.ANY), vmem),
        scratch_shapes=[pltpu.VMEM(x.shape, x.dtype) for x in ordered] + [
            pltpu.SMEM((kernels,), F32),
            pltpu.VMEM((rows + 2 * HALO, 2 * col_freqs), BF),
            pltpu.VMEM((3, 2 * SITES, cap), F32),
            pltpu.VMEM((3, 2 * SITES, cap), F32),
            pltpu.VMEM((rows, coarse), BF),
            pltpu.VMEM((2, REACH, coarse), F32),
            pltpu.VMEM((2, REACH, coarse), F32),
            pltpu.VMEM((3, 8, cap), F32),
            pltpu.VMEM((3, 8, cap), F32),
            pltpu.VMEM((3 * cap, frags), BF),
            pltpu.VMEM((rows, cols), F32),
            pltpu.VMEM((cols, rows), BF),
            pltpu.SemaphoreType.DMA((len(ordered) + 2,)),
            pltpu.SemaphoreType.DMA((4, 2)),
            pltpu.SemaphoreType.DMA((4, 2)),
        ],
        compiler_params=pltpu.CompilerParams(
            collective_id=0, has_side_effects=True, vmem_limit_bytes=63 << 20),
    )(kernel_weights, *ordered)
    new_bias = 0.5 * bias_steps.astype(F32) - 2.0 * (mean - threshold[0])
    return resist, new_bias


def solution(mesh):
    placed = (
        P(("groups", "tx"), None),
        P(),
        P(),
        P(),
        P(("groups", "tx")),
        P(None, None, ("groups", "tx")),
        P(("groups", "tx")),
    )
    return jax.shard_map(
        shards,
        mesh=mesh,
        in_specs=placed,
        out_specs=(P(("groups", "tx"), None), P(("groups", "tx"))),
        check_vma=False,
    )
```

```python
import math

import jax
import jax.numpy as jnp
import ml_dtypes
import numpy as np
from jax import lax
from jax.experimental import pallas as pl
from jax.experimental.pallas import tpu as pltpu
from jax.sharding import PartitionSpec as P

HALO = 256
REACH = 8
SITES = 16
GRID_STEP = 4
BLOCK = 64
SIGMA = 3.0
BF = jnp.bfloat16
F32 = jnp.float32
MESH = pl.DeviceIdType.MESH
LOADED = ("mask", "colf", "ev", "sc", "rowf", "ks", "rinv", "cinv", "rmid", "redge", "wide_t")


def host_bf16(x):
    return np.asarray(x, np.float32).astype(ml_dtypes.bfloat16)


def twiddle(position, frequency, period, amplitude):
    index = (position[:, None] * frequency[None, :]) % period
    angle = index.astype(np.float64) * (2.0 * math.pi / period)
    return np.cos(angle) * amplitude, np.sin(angle) * amplitude


def gauss(offset):
    every = np.arange(-REACH, REACH + 1)
    norm = np.sum(np.exp(-every * every / (2.0 * SIGMA * SIGMA)))
    value = np.exp(-offset * offset / (2.0 * SIGMA * SIGMA)) / norm
    return np.where(np.abs(offset) <= REACH, value, 0.0)


def split2(x):
    high = host_bf16(x)
    low = host_bf16(x - high.astype(np.float64))
    return high, low


def tables(rows, cols, row_freqs, col_freqs):
    window = rows + 2 * HALO
    f = np.arange(col_freqs) - col_freqs // 2
    g = np.arange(row_freqs) - row_freqs // 2
    c, s = twiddle(np.arange(cols), f, cols, 1.0 / math.sqrt(cols))
    col_forward = host_bf16(np.concatenate([c, -s], 1))
    c, s = twiddle(g, np.arange(window), window, 1.0 / math.sqrt(window))
    row_forward = host_bf16(np.concatenate([c, -s], 0))
    c, s = twiddle(np.arange(rows) + HALO, g, window, 1.0 / math.sqrt(row_freqs))
    row_inverse = host_bf16(np.block([[c, -s], [s, c]]))
    picked = np.arange(0, cols, GRID_STEP)
    c, s = twiddle(f, picked, cols, 1.0 / math.sqrt(col_freqs))
    col_inverse = host_bf16(np.block([[c, s], [-s, c]]))
    diff = np.arange(cols)[None, :] - picked[:, None]
    order = np.arange(1, col_freqs)
    base = np.arange(cols)
    kernel = 1.0 + 2.0 * np.cos(2 * math.pi * ((base[:, None] * order[None, :]) % cols) / cols).sum(1)
    kernel = (kernel + np.cos(2 * math.pi * ((base * col_freqs) % cols) / cols)) / picked.size
    interp = kernel[diff % cols]
    lines = np.arange(cols)
    col_blur = host_bf16(gauss((lines[None, :] - lines[:, None]).astype(np.float64)))
    spread = interp @ col_blur.astype(np.float64)
    high, low = split2(spread)
    wide = np.concatenate([high, low], 0)
    row_diff = np.arange(rows + 2 * REACH)[None, :] - REACH - np.arange(rows)[:, None]
    row_blur = host_bf16(gauss(row_diff.astype(np.float64)))
    row_mid = np.ascontiguousarray(row_blur[:, REACH:REACH + rows])
    row_edge = np.concatenate([row_blur[:, :REACH], row_blur[:, REACH + rows:]], 1)
    return (col_forward, row_forward, row_inverse, col_inverse, row_mid, row_edge, wide,
            np.ascontiguousarray(high.T))


def dot(a, b):
    return jnp.dot(a, b, preferred_element_type=F32)


def dot_nt(a, b):
    return lax.dot_general(a, b, (((1,), (1,)), ((), ())), preferred_element_type=F32)


def split3(x):
    high = x.astype(BF)
    rest = x - high.astype(F32)
    mid = rest.astype(BF)
    low = (rest - mid.astype(F32)).astype(BF)
    return jnp.concatenate([high, mid, low], axis=0)


def hat(distance):
    return jnp.maximum(1.0 - jnp.abs(distance), 0.0)


def kernel(weights_h, *refs):
    n = len(LOADED)
    sources = dict(zip(LOADED, refs[:n]))
    tile_h, mean_out = refs[n:n + 2]
    held = dict(zip(LOADED, refs[n + 2:2 * n + 2]))
    (weights, win, snd, recs, inten, hsnd, halo, rsnd, ret, sel, tile, rt,
     local_sem, send_sem, recv_sem) = refs[2 * n + 2:]
    mask, colf, ev, sc, rowf, ksv, rinv, cinv, rmid, redge, wide_t = (held[k] for k in LOADED)
    t = lax.axis_index("tx")
    count = lax.axis_size("tx")
    has_left = t > 0
    has_right = t < count - 1
    rows, cols = mask.shape
    coarse = cols // GRID_STEP
    kernels, row_freqs, col_freqs = ksv.shape[1:]
    frags = ev.shape[1]
    cap = frags // 2

    barrier = pltpu.get_barrier_semaphore()

    @pl.when(has_left)
    def _():
        pl.semaphore_signal(barrier, inc=1, device_id={"tx": t - 1}, device_id_type=MESH)

    @pl.when(has_right)
    def _():
        pl.semaphore_signal(barrier, inc=1, device_id={"tx": t + 1}, device_id_type=MESH)

    loads = {k: pltpu.make_async_copy(sources[k], held[k], local_sem.at[i])
             for i, k in enumerate(LOADED)}
    for k in LOADED:
        loads[k].start()
    load_weights = pltpu.make_async_copy(weights_h, weights, local_sem.at[n])
    load_weights.start()

    def to_left(kind, src, dst):
        return pltpu.make_async_remote_copy(
            src_ref=src, dst_ref=dst, send_sem=send_sem.at[kind, 0], recv_sem=recv_sem.at[kind, 0],
            device_id={"tx": t - 1}, device_id_type=MESH)

    def to_right(kind, src, dst):
        return pltpu.make_async_remote_copy(
            src_ref=src, dst_ref=dst, send_sem=send_sem.at[kind, 1], recv_sem=recv_sem.at[kind, 1],
            device_id={"tx": t + 1}, device_id_type=MESH)

    own = win.at[pl.ds(HALO, rows)]
    pairs = (
        (to_left(0, own, win.at[pl.ds(HALO + rows, HALO)]), to_right(0, own, win.at[pl.ds(0, HALO)])),
        (to_left(1, snd.at[0], recs.at[2]), to_right(1, snd.at[2], recs.at[0])),
        (to_left(2, hsnd.at[0], halo.at[1]), to_right(2, hsnd.at[1], halo.at[0])),
        (to_left(3, rsnd.at[0], ret.at[2]), to_right(3, rsnd.at[2], ret.at[0])),
    )

    def start(kind):
        @pl.when(has_left)
        def _():
            pairs[kind][0].start()

        @pl.when(has_right)
        def _():
            pairs[kind][1].start()

    def arrive(kind):
        @pl.when(has_right)
        def _():
            pairs[kind][0].wait_recv()

        @pl.when(has_left)
        def _():
            pairs[kind][1].wait_recv()

    @pl.when(jnp.logical_not(has_left))
    def _():
        win[0:HALO] = jnp.zeros((HALO, win.shape[1]), BF)
        recs[0] = jnp.zeros(recs.shape[1:], F32)
        halo[0] = jnp.zeros(halo.shape[1:], F32)
        ret[0] = jnp.zeros(ret.shape[1:], F32)

    @pl.when(jnp.logical_not(has_right))
    def _():
        win[HALO + rows:] = jnp.zeros((HALO, win.shape[1]), BF)
        recs[2] = jnp.zeros(recs.shape[1:], F32)
        halo[1] = jnp.zeros(halo.shape[1:], F32)
        ret[2] = jnp.zeros(ret.shape[1:], F32)

    loads["mask"].wait()
    loads["colf"].wait()
    win[HALO:HALO + rows] = dot(mask[...], colf[...]).astype(BF)

    between = jnp.logical_and(has_left, has_right)

    @pl.when(between)
    def _():
        pl.semaphore_wait(barrier, 2)

    @pl.when(jnp.logical_not(between))
    def _():
        pl.semaphore_wait(barrier, 1)

    start(0)

    loads["ev"].wait()
    loads["sc"].wait()
    offset = ev[...] - t + 1
    member = jnp.where(lax.broadcasted_iota(jnp.int32, (8, frags), 0) == offset, 1.0, 0.0)
    upper = jnp.where(
        lax.broadcasted_iota(jnp.int32, (frags, frags), 0)
        <= lax.broadcasted_iota(jnp.int32, (frags, frags), 1), 1.0, 0.0).astype(BF)
    inclusive = dot(member.astype(BF), upper)
    rank = jnp.sum(member * (inclusive - 1.0), axis=0, keepdims=True)
    slot = offset.astype(F32) * float(cap) + rank
    slot_line = lax.broadcasted_iota(jnp.int32, (3 * cap, frags), 0).astype(F32)
    sel[...] = jnp.where(slot_line == slot, 1.0, 0.0).astype(BF)
    records = jnp.concatenate([sc[0], sc[1]], axis=0)
    packed = dot_nt(split3(records), sel[...])
    n_rec = 2 * SITES
    packed = packed[:n_rec] + packed[n_rec:2 * n_rec] + packed[2 * n_rec:]
    snd[0] = packed[:, :cap]
    recs[1] = packed[:, cap:2 * cap]
    snd[2] = packed[:, 2 * cap:]
    start(1)

    loads["rowf"].wait()
    product = dot(rowf[:, HALO:HALO + rows], win[HALO:HALO + rows])
    for k in ("ks", "rinv", "cinv", "rmid", "redge"):
        loads[k].wait()
    load_weights.wait()
    arrive(0)
    product = product + dot(rowf[:, :HALO], win[:HALO]) + dot(rowf[:, HALO + rows:], win[HALO + rows:])
    real = product[:row_freqs, :col_freqs] - product[row_freqs:, col_freqs:]
    imag = product[:row_freqs, col_freqs:] + product[row_freqs:, :col_freqs]

    total = jnp.zeros((rows, cinv.shape[1] // 2), F32)
    half = cinv.shape[1] // 2
    for pair in range(kernels // 2):
        blocks = []
        for k in (2 * pair, 2 * pair + 1):
            kr = ksv[0, k]
            ki = ksv[1, k]
            blocks.append(jnp.concatenate(
                [(kr * real - ki * imag).astype(BF), (kr * imag + ki * real).astype(BF)], axis=0))
        field = dot(rinv[...], jnp.concatenate(blocks, axis=1)).astype(BF)
        for i in range(2):
            part = field[:, i * col_freqs:(i + 1) * col_freqs]
            e = dot(jnp.concatenate([part[:rows], part[rows:]], axis=1), cinv[...])
            er = e[:, :half]
            ei = e[:, half:]
            total = total + weights[2 * pair + i] * (er * er + ei * ei)

    rounded = total.astype(BF)
    inten[...] = rounded
    hsnd[0] = rounded[:REACH].astype(F32)
    hsnd[1] = rounded[rows - REACH:].astype(F32)
    start(2)
    blurred = dot(rmid[...], inten[...])
    arrive(2)
    edge = jnp.concatenate([halo[0], halo[1]], axis=0).astype(BF)
    blurred = blurred + dot(redge[...], edge)
    center = jnp.sum(blurred) * (1.0 / (blurred.shape[0] * blurred.shape[1]))
    high = blurred.astype(BF)
    low = (blurred - high.astype(F32)).astype(BF)
    loads["wide_t"].wait()
    rt[...] = (dot_nt(wide_t[...], high) + dot_nt(wide_t[...], low) - center).astype(BF)
    tile[:, :coarse] = high
    tile[:, coarse:] = low
    store = pltpu.make_async_copy(tile, tile_h, local_sem.at[n + 1])
    store.start()
    arrive(1)

    blocks_n = cols // BLOCK
    row_line = lax.broadcasted_iota(jnp.int32, (rows, cap), 0).astype(F32)
    col_line = lax.broadcasted_iota(jnp.int32, (BLOCK, cap), 0).astype(F32)
    end_line = lax.broadcasted_iota(jnp.int32, (8, cap), 0).astype(F32) + float(BLOCK)

    def evaluate(block):
        def one(s, acc):
            p = recs[block, pl.ds(s, 1), :] * float(rows - 1)
            q = recs[block, pl.ds(SITES + s, 1), :] * float(cols - 1)
            wr = hat(row_line - p).astype(BF)
            lines = dot(rt[...], wr)
            h = jnp.floor(q * (1.0 / BLOCK))
            local = q - h * float(BLOCK)
            chosen = lines[:BLOCK]
            after = jnp.zeros((8, cap), F32)
            for k in range(1, blocks_n):
                here = lines[k * BLOCK:(k + 1) * BLOCK]
                chosen = jnp.where(h == float(k), here, chosen)
                after = jnp.where(h == float(k - 1), here[:8], after)
            weighted = chosen * hat(col_line - local)
            for g in range(BLOCK // 8):
                acc = acc + weighted[g * 8:(g + 1) * 8]
            return acc + after * hat(end_line - local)

        def step(i, acc):
            for j in range(8):
                acc = one(8 * i + j, acc)
            return acc

        acc = lax.fori_loop(0, SITES // 8, step, jnp.zeros((8, cap), F32))
        mean = jnp.sum(acc, axis=0, keepdims=True) * (1.0 / SITES) + center
        return jnp.broadcast_to(mean, (8, cap))

    rsnd[0] = evaluate(0)
    rsnd[2] = evaluate(2)
    start(3)
    ret[1] = evaluate(1)
    arrive(3)
    back = jnp.concatenate([ret[0], ret[1], ret[2]], axis=1)
    found = dot(split3(back), sel[...])
    mean_out[...] = (found[0:1] + found[8:9] + found[16:17]).reshape(frags)

    for kind in range(4):
        @pl.when(has_left)
        def _():
            pairs[kind][0].wait_send()

        @pl.when(has_right)
        def _():
            pairs[kind][1].wait_send()
    store.wait()


def finish(tile, wide, mean, bias, thresh, resist, nb):
    coarse = wide.shape[0] // 2
    high = tile[:, :coarse]
    low = tile[:, coarse:]
    upper = wide[:coarse]
    resist[...] = (dot(high, upper) + dot(low, upper)) + dot(high, wide[coarse:])

    @pl.when(pl.program_id(0) == 0)
    def _():
        nb[...] = 0.5 * bias[...].astype(F32) - 2.0 * (mean[...] - thresh[0])


def shards(mask, kernel_spectra, kernel_weights, threshold, eval_tile, site_coords, bias_steps):
    rows, cols = mask.shape
    row_freqs, kernels, col_freqs = kernel_spectra.shape[1:]
    frags = eval_tile.shape[0]
    cap = frags // 2
    names = ("colf", "rowf", "rinv", "cinv", "rmid", "redge", "wide", "wide_t")
    values = dict(zip(names, (jnp.asarray(x) for x in tables(rows, cols, row_freqs, col_freqs))))
    values["mask"] = mask
    values["ks"] = jnp.transpose(kernel_spectra, (0, 2, 1, 3))
    values["ev"] = eval_tile.reshape(1, frags)
    values["sc"] = site_coords
    ordered = [values[k] for k in LOADED]
    vmem = pl.BlockSpec(memory_space=pltpu.VMEM)
    hbm = pl.BlockSpec(memory_space=pltpu.HBM)
    coarse = cols // GRID_STEP
    tile, mean = pl.pallas_call(
        kernel,
        out_shape=(jax.ShapeDtypeStruct((rows, 2 * coarse), BF), jax.ShapeDtypeStruct((frags,), F32)),
        in_specs=[hbm] * (1 + len(ordered)),
        out_specs=(pl.BlockSpec(memory_space=pl.ANY), vmem),
        scratch_shapes=[pltpu.VMEM(x.shape, x.dtype) for x in ordered] + [
            pltpu.SMEM((kernels,), F32),
            pltpu.VMEM((rows + 2 * HALO, 2 * col_freqs), BF),
            pltpu.VMEM((3, 2 * SITES, cap), F32),
            pltpu.VMEM((3, 2 * SITES, cap), F32),
            pltpu.VMEM((rows, coarse), BF),
            pltpu.VMEM((2, REACH, coarse), F32),
            pltpu.VMEM((2, REACH, coarse), F32),
            pltpu.VMEM((3, 8, cap), F32),
            pltpu.VMEM((3, 8, cap), F32),
            pltpu.VMEM((3 * cap, frags), BF),
            pltpu.VMEM((rows, 2 * coarse), BF),
            pltpu.VMEM((cols, rows), BF),
            pltpu.SemaphoreType.DMA((len(ordered) + 2,)),
            pltpu.SemaphoreType.DMA((4, 2)),
            pltpu.SemaphoreType.DMA((4, 2)),
        ],
        compiler_params=pltpu.CompilerParams(
            collective_id=0, has_side_effects=True, vmem_limit_bytes=63 << 20),
    )(kernel_weights, *ordered)
    parts = 2
    whole = lambda i: (0,)
    resist, new_bias = pl.pallas_call(
        finish,
        grid=(parts,),
        out_shape=(jax.ShapeDtypeStruct((rows, cols), F32), jax.ShapeDtypeStruct((frags,), F32)),
        in_specs=[
            pl.BlockSpec((rows, 2 * coarse), lambda i: (0, 0)),
            pl.BlockSpec((2 * coarse, cols // parts), lambda i: (0, i)),
            pl.BlockSpec((frags,), whole),
            pl.BlockSpec((frags,), whole),
            pl.BlockSpec(memory_space=pltpu.SMEM),
        ],
        out_specs=(pl.BlockSpec((rows, cols // parts), lambda i: (0, i)), pl.BlockSpec((frags,), whole)),
    )(tile, values["wide"], mean, bias_steps, threshold)
    return resist, new_bias


def solution(mesh):
    placed = (
        P(("groups", "tx"), None),
        P(),
        P(),
        P(),
        P(("groups", "tx")),
        P(None, None, ("groups", "tx")),
        P(("groups", "tx")),
    )
    return jax.shard_map(
        shards,
        mesh=mesh,
        in_specs=placed,
        out_specs=(P(("groups", "tx"), None), P(("groups", "tx"))),
        check_vma=False,
    )
```
